32 devices in a mesh: fsdp: 16 (over z, y, core), ctx: 2 (over x).
Axes of the slice: x: 2, y: 2, z: 4, core: 2. Of those that a mesh axis runs over, the one named last changes fastest.
Arguments:
- tokens: bfloat16 [16, 512, 384], P('fsdp', 'ctx'), may hold values from -6 to 6
- condition: bfloat16 [16, 384], P('fsdp'), may hold values from -6 to 6
- ada_weight: bfloat16 [384, 2304], P('fsdp'), may hold values from -0.3125 to 0.3125
- ada_bias: bfloat16 [2304], P('fsdp'), may hold values from -5 to 5
- qkv_weight: bfloat16 [384, 1152], P('fsdp'), may hold values from -1 to 1
- qv_bias: bfloat16 [768], P('fsdp'), may hold values from -5 to 5
- out_weight: bfloat16 [384, 384], P('fsdp'), may hold values from -2.5 to 2.5
- out_bias: bfloat16 [384], P('fsdp'), may hold values from -5 to 5
- fc1_weight: bfloat16 [384, 1536], P('fsdp'), may hold values from -0.3125 to 0.3125
- fc1_bias: bfloat16 [1536], P('fsdp'), may hold values from -5 to 5
- fc2_weight: bfloat16 [1536, 384], P('fsdp'), may hold values from -0.15625 to 0.15625
- fc2_bias: bfloat16 [384], P('fsdp'), may hold values from -5 to 5
- cotangent: bfloat16 [16, 512, 384], P('fsdp', 'ctx'), may hold values from -6 to 6
Outputs:
- output: bfloat16 [16, 512, 384], P('fsdp', 'ctx')
- grad_tokens: bfloat16 [16, 512, 384], P('fsdp', 'ctx')
- grad_condition: float32 [16, 384], P('fsdp')
- grad_ada_weight: float32 [384, 2304], P('fsdp')
- grad_ada_bias: float32 [2304], P('fsdp')
- grad_qkv_weight: float32 [384, 1152], P('fsdp')
- grad_qv_bias: float32 [768], P('fsdp')
- grad_out_weight: float32 [384, 384], P('fsdp')
- grad_out_bias: float32 [384], P('fsdp')
- grad_fc1_weight: float32 [384, 1536], P('fsdp')
- grad_fc1_bias: float32 [1536], P('fsdp')
- grad_fc2_weight: float32 [1536, 384], P('fsdp')
- grad_fc2_bias: float32 [384], P('fsdp')
The draws below stay inside these ranges and needn't reach their ends.
All inputs are finite; a program needn't handle non-finite values.
Results may differ from the reference program's by a relative error of at most 0.022.
Values may be sent and summed in bfloat16 or wider, within the bound.
A program may use at most 64 MiB of HBM per device.

```python
from functools import partial
import jax
import jax.numpy as jnp
from jax import lax

D = 384
HEADS = 6
HEAD = 64
FF = 1536
COND = 384
LENGTH = 512
BATCH = 16


def draw_qkv_weight(key, part):
    first = jax.random.fold_in(jax.random.fold_in(key, 17), 0)
    base = jax.random.normal(first, (D, 3 * D), jnp.float32) * D ** (-0.5)
    return jnp.clip(base, -1.0, 1.0).astype(jnp.bfloat16)


def shard_levels(key, dims, shards, low, largest):
    loudness, own = 1.0, jax.random.fold_in(key, 6)
    for position, parts in shards:
        heights = jnp.exp(jax.random.uniform(jax.random.fold_in(own, position), (parts,), jnp.float32, low / len(shards), largest / len(shards)))
        loudness = loudness * jnp.repeat(heights, dims[position] // parts).reshape([-1 if axis == position else 1 for axis in range(len(dims))])
    return loudness


def gaussian(key, extent, spread, limit, pieces=(), dtype=jnp.bfloat16):
    values = jax.random.normal(key, extent, jnp.float32) * spread
    if len(pieces) > 0:
        values = shard_levels(key, extent, pieces, -0.22, 0.18) * values
    return jnp.clip(values, min=-limit, max=limit).astype(dtype)


def setup_inputs(seed: int = 0) -> dict:
    key_of = jax.random.split(jax.random.key(seed), 14)
    tokens = gaussian(key_of[0], (BATCH, LENGTH, D), 1.0, 6.0, ((0, 16), (1, 2)))
    condition = gaussian(key_of[1], (BATCH, COND), 1.0, 6.0, ((0, 16),))
    ada_weight = gaussian(key_of[2], (COND, 6 * D), COND ** -0.5, 0.3125, ((0, 16),))
    ada_bias = gaussian(key_of[3], (6 * D,), 1.0, 5.0, ((0, 16),))
    qkv_weight = draw_qkv_weight(jax.random.fold_in(key_of[13], 71), 0)
    qv_bias = gaussian(key_of[5], (2 * D,), 1.0, 5.0, ((0, 16),))
    out_weight = gaussian(key_of[6], (D, D), (D // 64) ** -0.5, 2.5, ((0, 16),))
    out_bias = gaussian(key_of[7], (D,), 1.0, 5.0, ((0, 16),))
    fc1_weight = gaussian(key_of[8], (D, FF), D ** -0.5, 0.3125, ((0, 16),))
    fc1_bias = gaussian(key_of[9], (FF,), 1.0, 5.0, ((0, 16),))
    fc2_weight = gaussian(key_of[10], (FF, D), FF ** -0.5, 0.15625, ((0, 16),))
    fc2_bias = gaussian(key_of[11], (D,), 1.0, 5.0, ((0, 16),))
    cotangent = gaussian(key_of[12], (BATCH, LENGTH, D), 1.0, 6.0, ((0, 16), (1, 2)))
    return {"tokens": tokens, "condition": condition, "ada_weight": ada_weight, "ada_bias": ada_bias, "qkv_weight": qkv_weight, "qv_bias": qv_bias, "out_weight": out_weight, "out_bias": out_bias, "fc1_weight": fc1_weight, "fc1_bias": fc1_bias, "fc2_weight": fc2_weight, "fc2_bias": fc2_bias, "cotangent": cotangent}


epsilon = 1e-06

def layer_stats(values):
    centered = values - lax.optimization_barrier(jnp.mean(values, axis=-1, keepdims=True))
    inverse = lax.rsqrt(lax.optimization_barrier(jnp.mean(centered * centered, axis=-1, keepdims=True)) + epsilon)
    return (centered * inverse, inverse)

def layer_back(normed, inverse, grad_normed):
    mean_grad = lax.optimization_barrier(jnp.mean(grad_normed, axis=-1, keepdims=True))
    mean_prod = lax.optimization_barrier(jnp.mean(grad_normed * normed, axis=-1, keepdims=True))
    return inverse * (grad_normed - mean_grad - normed * mean_prod)

def gelu_back(hidden, grad_output):
    return jax.vjp(partial(jax.nn.gelu, approximate=True), hidden)[1](grad_output)[0]

def matmul(left, right):
    return jnp.dot(left, right, preferred_element_type=jnp.float32)

def split_heads(array):
    return array.reshape(LENGTH, HEADS, HEAD).transpose(1, 0, 2)

def merge_heads(array):
    return array.transpose(1, 0, 2).reshape(LENGTH, D)

def reference(tokens, condition, ada_weight, ada_bias, qkv_weight, qv_bias, out_weight, out_bias, fc1_weight, fc1_bias, fc2_weight, fc2_bias, cotangent):
    scale_factor = HEAD ** (-0.5)

    def head_forward(operands):
        query_head, key_head, value_head = operands
        scores = matmul(query_head, key_head.T) * scale_factor
        highest = lax.optimization_barrier(jnp.max(scores, axis=1, keepdims=True))
        log_total = highest + jnp.log(lax.optimization_barrier(jnp.sum(jnp.exp(scores - highest), axis=1, keepdims=True)))
        weights = jnp.exp(scores - log_total).astype(jnp.bfloat16)
        mixed_head = matmul(weights, value_head).astype(jnp.bfloat16)
        return (mixed_head, log_total[:, 0])

    def head_backward(operands):
        query_head, key_head, value_head, mixed_head, grad_head, log_total = operands
        scores = matmul(query_head, key_head.T) * scale_factor
        probability = jnp.exp(scores - log_total[:, None])
        prob_half = probability.astype(jnp.bfloat16)
        grad_value = matmul(prob_half.T, grad_head)
        grad_prob = matmul(grad_head, value_head.T)
        row_inner = lax.optimization_barrier(jnp.sum(grad_head.astype(jnp.float32) * mixed_head.astype(jnp.float32), axis=1, keepdims=True))
        grad_scores = (probability * (grad_prob - row_inner) * scale_factor).astype(jnp.bfloat16)
        grad_query = matmul(grad_scores, key_head)
        grad_key = matmul(grad_scores.T, query_head)
        return (grad_query, grad_key, grad_value)

    def latent_step(totals, inputs):
        token_rows, cond_row, cot_rows = inputs
        cond_float = cond_row.astype(jnp.float32)[None, :]
        cond_silu = jax.nn.silu(cond_float).astype(jnp.bfloat16)
        modulation = matmul(cond_silu, ada_weight) + ada_bias.astype(jnp.float32)[None, :]
        shift_one, scale_one, gate_one, shift_two, scale_two, gate_two = jnp.split(modulation, 6, axis=1)
        residual = token_rows.astype(jnp.float32)
        normed_one, inverse_one = layer_stats(residual)
        hidden_one = (normed_one * (1.0 + scale_one) + shift_one).astype(jnp.bfloat16)
        projected = matmul(hidden_one, qkv_weight)
        bias_float = qv_bias.astype(jnp.float32)
        queries = (projected[:, :D] + bias_float[:D]).astype(jnp.bfloat16)
        keys = projected[:, D:2 * D].astype(jnp.bfloat16)
        values = (projected[:, 2 * D:] + bias_float[D:]).astype(jnp.bfloat16)
        heads_query = split_heads(queries)
        heads_key = split_heads(keys)
        heads_value = split_heads(values)
        mixed_heads, log_totals = lax.map(head_forward, (heads_query, heads_key, heads_value))
        mixed = merge_heads(mixed_heads)
        attn_out = matmul(mixed, out_weight) + out_bias.astype(jnp.float32)
        after_attn = residual + gate_one * attn_out
        normed_two, inverse_two = layer_stats(after_attn)
        hidden_two = (normed_two * (1.0 + scale_two) + shift_two).astype(jnp.bfloat16)
        pre_act = matmul(hidden_two, fc1_weight) + fc1_bias.astype(jnp.float32)
        activated = jax.nn.gelu(pre_act, approximate=True).astype(jnp.bfloat16)
        mlp_out = matmul(activated, fc2_weight) + fc2_bias.astype(jnp.float32)
        result = (after_attn + gate_two * mlp_out).astype(jnp.bfloat16)
        grad_result = cot_rows.astype(jnp.float32)
        grad_gate_two = lax.optimization_barrier(jnp.sum(grad_result * mlp_out, axis=0, keepdims=True))
        grad_mlp_float = grad_result * gate_two
        grad_mlp = grad_mlp_float.astype(jnp.bfloat16)
        grad_fc2_w = matmul(activated.T, grad_mlp)
        grad_fc2_b = lax.optimization_barrier(jnp.sum(grad_mlp_float, axis=0))
        grad_pre = gelu_back(pre_act, matmul(grad_mlp, fc2_weight.T))
        grad_pre_half = grad_pre.astype(jnp.bfloat16)
        grad_fc1_w = matmul(hidden_two.T, grad_pre_half)
        grad_fc1_b = lax.optimization_barrier(jnp.sum(grad_pre, axis=0))
        grad_hidden_two = matmul(grad_pre_half, fc1_weight.T)
        grad_scale_two = lax.optimization_barrier(jnp.sum(grad_hidden_two * normed_two, axis=0, keepdims=True))
        grad_shift_two = lax.optimization_barrier(jnp.sum(grad_hidden_two, axis=0, keepdims=True))
        grad_after = grad_result + layer_back(normed_two, inverse_two, grad_hidden_two * (1.0 + scale_two))
        grad_gate_one = lax.optimization_barrier(jnp.sum(grad_after * attn_out, axis=0, keepdims=True))
        grad_attn_float = grad_after * gate_one
        grad_attn = grad_attn_float.astype(jnp.bfloat16)
        grad_out_w = matmul(mixed.T, grad_attn)
        grad_out_b = lax.optimization_barrier(jnp.sum(grad_attn_float, axis=0))
        grad_mixed = matmul(grad_attn, out_weight.T).astype(jnp.bfloat16)
        grad_q_heads, grad_k_heads, grad_v_heads = lax.map(head_backward, (heads_query, heads_key, heads_value, mixed_heads, split_heads(grad_mixed), log_totals))
        grad_query = merge_heads(grad_q_heads)
        grad_value = merge_heads(grad_v_heads)
        grad_projected = jnp.concatenate([grad_query, merge_heads(grad_k_heads), grad_value], axis=1).astype(jnp.bfloat16)
        grad_qkv_w = matmul(hidden_one.T, grad_projected)
        grad_qv_b = jnp.concatenate([lax.optimization_barrier(jnp.sum(grad_query, axis=0)), lax.optimization_barrier(jnp.sum(grad_value, axis=0))])
        grad_hidden_one = matmul(grad_projected, qkv_weight.T)
        grad_scale_one = lax.optimization_barrier(jnp.sum(grad_hidden_one * normed_one, axis=0, keepdims=True))
        grad_shift_one = lax.optimization_barrier(jnp.sum(grad_hidden_one, axis=0, keepdims=True))
        grad_input = (grad_after + layer_back(normed_one, inverse_one, grad_hidden_one * (1.0 + scale_one))).astype(jnp.bfloat16)
        grad_mod = jnp.concatenate([grad_shift_one, grad_scale_one, grad_gate_one, grad_shift_two, grad_scale_two, grad_gate_two], axis=1)
        grad_ada_w = jnp.dot(cond_silu.astype(jnp.float32).T, grad_mod, precision=lax.Precision.HIGHEST)
        grad_ada_b = grad_mod[0]
        ada_back_term = jnp.dot(grad_mod, ada_weight.astype(jnp.float32).T, precision=lax.Precision.HIGHEST)
        grad_cond = jax.vjp(jax.nn.silu, cond_float)[1](ada_back_term)[0][0]
        updates = (grad_ada_w, grad_ada_b, grad_qkv_w, grad_qv_b, grad_out_w, grad_out_b, grad_fc1_w, grad_fc1_b, grad_fc2_w, grad_fc2_b)
        totals = tuple((running + update for running, update in zip(totals, updates)))
        return (totals, (result, grad_input, grad_cond))
    zeros_like = (jnp.zeros((COND, 6 * D), jnp.float32), jnp.zeros((6 * D,), jnp.float32), jnp.zeros((D, 3 * D), jnp.float32), jnp.zeros((2 * D,), jnp.float32), jnp.zeros((D, D), jnp.float32), jnp.zeros((D,), jnp.float32), jnp.zeros((D, FF), jnp.float32), jnp.zeros((FF,), jnp.float32), jnp.zeros((FF, D), jnp.float32), jnp.zeros((D,), jnp.float32))
    totals, stacked = lax.scan(latent_step, zeros_like, (tokens, condition, cotangent))
    result, grad_input, grad_cond = stacked
    return (result, grad_input, grad_cond, totals[0], totals[1], totals[2], totals[3], totals[4], totals[5], totals[6], totals[7], totals[8], totals[9])
```

```python
from functools import partial

import jax
import jax.numpy as jnp
from jax import lax
from jax.experimental import pallas as pl
from jax.experimental.pallas import tpu as pltpu
from jax.sharding import PartitionSpec as P

HEADS = 6
HEAD = 64
MESH = pl.DeviceIdType.MESH
F32 = jnp.float32
BF16 = jnp.bfloat16


epsilon = 1e-06


def layer_stats(values):
    centered = values - jnp.mean(values, axis=-1, keepdims=True)
    inverse = lax.rsqrt(jnp.mean(centered * centered, axis=-1, keepdims=True) + epsilon)
    return (centered * inverse, inverse)


def layer_back(normed, inverse, grad_normed):
    mean_grad = jnp.mean(grad_normed, axis=-1, keepdims=True)
    mean_prod = jnp.mean(grad_normed * normed, axis=-1, keepdims=True)
    return inverse * (grad_normed - mean_grad - normed * mean_prod)


def gelu_back(hidden, grad_output):
    return jax.vjp(partial(jax.nn.gelu, approximate=True), hidden)[1](grad_output)[0]


def matmul(left, right):
    return jnp.dot(left, right, preferred_element_type=F32)


def matmul_nt(left, right):
    return lax.dot_general(left, right, (((1,), (1,)), ((), ())), preferred_element_type=F32)


def matmul_tn(left, right):
    return lax.dot_general(left, right, (((0,), (0,)), ((), ())), preferred_element_type=F32)


def flip(index, mask):
    return index + mask - 2 * mask * ((index // mask) % 2)


def loop(count, body):
    def step(i, carry):
        body(i)
        return carry

    lax.fori_loop(0, count, step, 0)


def remote(src, dst, send, recv, **device):
    return pltpu.make_async_remote_copy(
        src_ref=src, dst_ref=dst, send_sem=send, recv_sem=recv,
        device_id=device, device_id_type=MESH,
    )


def meet(n, c, me, row):
    barrier = pltpu.get_barrier_semaphore()

    def greet_fsdp(k):
        pl.semaphore_signal(
            barrier, inc=1, device_id={"fsdp": (me + 1 + k) % n}, device_id_type=MESH
        )

    def greet_ctx(k):
        pl.semaphore_signal(
            barrier, inc=1, device_id={"ctx": (row + 1 + k) % c}, device_id_type=MESH
        )

    loop(n - 1, greet_fsdp)
    loop(c - 1, greet_ctx)
    pl.semaphore_wait(barrier, n + c - 2)


def gather_kernel(
    n, c,
    qkv, out, fc1, fc2, tok, cond, ada, ada_bias, small,
    qkv_all, out_all, fc1_all, fc2_all, tok_all, cond_all, mod, small_all,
    part, mod_all,
    send_w, recv_w, send_t, recv_t, send_c, recv_c, send_m, recv_m, send_s, recv_s,
):
    me, row = lax.axis_index("fsdp"), lax.axis_index("ctx")
    own = (qkv, out, fc1, fc2)
    full = (qkv_all, out_all, fc1_all, fc2_all)
    stages = n.bit_length() - 1
    meet(n, c, me, row)

    def cond_copy(to, sender):
        return remote(
            cond.at[to], cond_all.at[sender], send_c.at[to], recv_c.at[sender], fsdp=to
        )

    def small_copy(to, sender):
        return remote(small, small_all.at[sender], send_s.at[to], recv_s.at[sender], fsdp=to)

    def mod_copy(to, sender):
        return remote(part.at[to], mod_all.at[sender], send_m.at[to], recv_m.at[sender], fsdp=to)

    def tok_copy(to, sender):
        return remote(tok, tok_all.at[sender], send_t.at[to], recv_t.at[sender], ctx=to)

    def weight_copy(w, s, block, mine):
        return remote(
            own[w] if mine else full[w].at[block],
            full[w].at[block],
            send_w.at[w, s, block],
            recv_w.at[w, block],
            fsdp=flip(me, n >> (s + 1)),
        )

    def others(body):
        loop(n - 1, lambda k: body((me + 1 + k) % n))

    def siblings(body):
        loop(c - 1, lambda k: body((row + 1 + k) % c))

    others(lambda to: cond_copy(to, me).start())
    for w in range(4):
        for s in range(stages):
            weight_copy(w, s, me, True).start()
    others(lambda to: small_copy(to, me).start())
    siblings(lambda to: tok_copy(to, row).start())
    for w in range(4):
        full[w][me] = own[w][...]
    tok_all[row] = tok[...]
    small_all[me] = small[...]
    cond_all[me] = cond[me]
    others(lambda peer: cond_copy(peer, peer).wait_recv())
    lane = lax.broadcasted_iota(jnp.int32, cond_all.shape[1:], 1)
    columns = jnp.zeros(cond_all.shape[1:], F32)
    for i in range(n):
        columns = jnp.where(lane == i, cond_all[i], columns)
    partial_mod = matmul_tn(columns.astype(BF16), ada[...])
    for i in range(n):
        part[i] = partial_mod[i : i + 1, :] + ada_bias[...]
    others(lambda to: mod_copy(to, me).start())
    mod_all[me] = part[me]

    for s in range(stages):
        mask = n >> (s + 1)
        origin = flip(me, mask) % (2 * mask)

        def arrived(t, s=s, mask=mask, origin=origin):
            block = origin + t * (2 * mask)
            for w in range(4):
                weight_copy(w, s, block, False).wait_recv()
                for later in range(s + 1, stages):
                    weight_copy(w, later, block, False).start()

        loop(1 << s, arrived)

    others(lambda peer: mod_copy(peer, peer).wait_recv())
    total = mod_all[0]
    for i in range(1, n):
        total = total + mod_all[i]
    mod[...] = total
    others(lambda peer: small_copy(peer, peer).wait_recv())
    siblings(lambda peer: tok_copy(peer, peer).wait_recv())
    for s in range(stages):
        mask = n >> (s + 1)

        def left(t, s=s, mask=mask):
            block = me % (2 * mask) + t * (2 * mask)
            for w in range(4):
                weight_copy(w, s, block, False).wait_send()

        loop(1 << s, left)
    others(lambda to: cond_copy(to, me).wait_send())
    others(lambda to: small_copy(to, me).wait_send())
    others(lambda to: mod_copy(to, me).wait_send())
    siblings(lambda to: tok_copy(to, row).wait_send())


def vmem(count):
    return [pl.BlockSpec(memory_space=pltpu.VMEM)] * count


def gather(n, c, qkv, out, fc1, fc2, tok, cond, ada, ada_bias, small):
    stages = n.bit_length() - 1
    shape = jax.ShapeDtypeStruct
    dma = pltpu.SemaphoreType.DMA
    return pl.pallas_call(
        partial(gather_kernel, n, c),
        out_shape=[shape((n, *w.shape), BF16) for w in (qkv, out, fc1, fc2)]
        + [
            shape((c, *tok.shape), BF16),
            shape(cond.shape, F32),
            shape(ada_bias.shape, F32),
            shape((n, *small.shape), F32),
        ],
        in_specs=vmem(9),
        out_specs=vmem(8),
        scratch_shapes=[
            pltpu.VMEM((n, *ada_bias.shape), F32),
            pltpu.VMEM((n, *ada_bias.shape), F32),
            dma((4, stages, n)), dma((4, n)),
            dma((c,)), dma((c,)), dma((n,)), dma((n,)), dma((n,)), dma((n,)), dma((n,)), dma((n,)),
        ],
        compiler_params=pltpu.CompilerParams(collective_id=0, has_side_effects=True),
        name="gather",
    )(qkv, out, fc1, fc2, tok, cond, ada, ada_bias, small)


def reduce_kernel(
    n, c,
    qkv, out, fc1, fc2, bias, gm, ada,
    qkv_sum, out_sum, fc1_sum, fc2_sum, bias_sum, gm_all, back_all,
    *scratch,
):
    stages = n.bit_length() - 1
    me, row = lax.axis_index("fsdp"), lax.axis_index("ctx")
    given = (qkv, out, fc1, fc2, bias)
    sums = (qkv_sum, out_sum, fc1_sum, fc2_sum, bias_sum)
    arrays = len(given)
    incoming = [scratch[w * stages : (w + 1) * stages] for w in range(arrays)]
    scratch = scratch[arrays * stages :]
    kept = [scratch[w * stages : (w + 1) * stages] for w in range(arrays)]
    scratch = scratch[arrays * stages :]
    shares, scratch = scratch[:arrays], scratch[arrays:]
    (gm_ctx, gm_mine, back, send_r, recv_r, send_x, recv_x, send_g, recv_g, send_f, recv_f,
     send_b, recv_b) = scratch
    meet(n, c, me, row)

    def others(body):
        loop(n - 1, lambda k: body((me + 1 + k) % n))

    def siblings(body):
        loop(c - 1, lambda k: body((row + 1 + k) % c))

    def ctx_gm(to, sender):
        return remote(gm, gm_ctx.at[sender], send_g.at[to], recv_g.at[sender], ctx=to)

    def fsdp_gm(to, sender):
        return remote(gm_mine, gm_all.at[sender], send_f.at[to], recv_f.at[sender], fsdp=to)

    def back_copy(to, sender):
        return remote(back.at[to], back_all.at[sender], send_b.at[to], recv_b.at[sender], fsdp=to)

    def share_copy(w, to, sender):
        return remote(
            shares[w].at[row], shares[w].at[sender], send_x.at[w, to], recv_x.at[w, sender], ctx=to
        )

    def bit(s):
        return (me // (1 << s)) % 2

    def source(w, s):
        return given[w] if s == 0 else kept[w][s - 1]

    def halve(w, s, j):
        return remote(
            source(w, s).at[2 * j + 1 - bit(s)],
            incoming[w][s].at[j],
            send_r.at[w, s, j],
            recv_r.at[w, s, j],
            fsdp=flip(me, 1 << s),
        )

    siblings(lambda to: ctx_gm(to, row).start())

    def send_all(s, base, step, count):
        def body(t):
            for w in range(arrays):
                halve(w, s, base + step * t).start()

        loop(count, body)

    send_all(0, 1 - bit(1), 2, n // 4)
    send_all(0, bit(1), 2, n // 4)

    gm_ctx[row] = gm[...]
    siblings(lambda peer: ctx_gm(peer, peer).wait_recv())
    total = gm_ctx[0]
    for i in range(1, c):
        total = total + gm_ctx[i]
    gm_mine[...] = total
    gm_all[me] = total
    others(lambda to: fsdp_gm(to, me).start())

    def backward():
        others(lambda peer: fsdp_gm(peer, peer).wait_recv())
        rows = lax.broadcasted_iota(jnp.int32, (n, gm.shape[1]), 0)
        stacked = jnp.zeros((n, gm.shape[1]), F32)
        for i in range(n):
            stacked = jnp.where(rows == i, jnp.broadcast_to(gm_all[i], stacked.shape), stacked)
        product = lax.dot_general(
            stacked, ada[...], (((1,), (1,)), ((), ())),
            preferred_element_type=F32, precision=lax.Precision.HIGHEST,
        )
        for i in range(n):
            back[i] = product[i : i + 1, :]
        others(lambda to: back_copy(to, me).start())
        back_all[me] = back[me]

    def add(w, s, j):
        halve(w, s, j).wait_recv()
        value = source(w, s)[2 * j + bit(s)].astype(F32) + incoming[w][s][j].astype(F32)
        if s == stages - 1:
            shares[w][row] = value.astype(given[w].dtype)
        else:
            kept[w][s][j] = value.astype(given[w].dtype)

    for s in range(stages):
        if s == stages - 1:
            for w in range(arrays):
                add(w, s, 0)
                siblings(lambda to, w=w: share_copy(w, to, row).start())
            continue

        def first(t, s=s):
            j = 2 * t + 1 - bit(s + 1)
            for w in range(arrays):
                add(w, s, j)
                halve(w, s + 1, t).start()

        def second(t, s=s):
            for w in range(arrays):
                add(w, s, 2 * t + bit(s + 1))

        loop(n >> (s + 2), first)
        loop(n >> (s + 2), second)
        if s == 0:
            backward()

    for w in range(arrays):
        siblings(lambda peer, w=w: share_copy(w, peer, peer).wait_recv())
        value = shares[w][0].astype(F32)
        for i in range(1, c):
            value = value + shares[w][i].astype(F32)
        sums[w][...] = value
    others(lambda peer: back_copy(peer, peer).wait_recv())

    siblings(lambda to: ctx_gm(to, row).wait_send())
    others(lambda to: fsdp_gm(to, me).wait_send())
    others(lambda to: back_copy(to, me).wait_send())
    for s in range(stages):

        def sent(j, s=s):
            for w in range(arrays):
                halve(w, s, j).wait_send()

        loop(n >> (s + 1), sent)
    for w in range(arrays):
        siblings(lambda to, w=w: share_copy(w, to, row).wait_send())


def reduce(n, c, qkv, out, fc1, fc2, bias, gm, ada):
    stages = n.bit_length() - 1
    shape = jax.ShapeDtypeStruct
    dma = pltpu.SemaphoreType.DMA
    given = (qkv, out, fc1, fc2, bias)
    halves = [
        pltpu.VMEM((n >> (s + 1), *w.shape[1:]), w.dtype) for w in given for s in range(stages)
    ]
    return pl.pallas_call(
        partial(reduce_kernel, n, c),
        out_shape=[shape(w.shape[1:], F32) for w in given]
        + [shape((n, *gm.shape), F32), shape((n, 1, ada.shape[0]), F32)],
        in_specs=vmem(7),
        out_specs=vmem(7),
        scratch_shapes=halves
        + halves
        + [pltpu.VMEM((c, *w.shape[1:]), w.dtype) for w in given]
        + [
            pltpu.VMEM((c, *gm.shape), F32),
            pltpu.VMEM(gm.shape, F32),
            pltpu.VMEM((n, 1, ada.shape[0]), F32),
            dma((5, stages, n // 2)), dma((5, stages, n // 2)),
            dma((5, c)), dma((5, c)), dma((c,)), dma((c,)),
            dma((n,)), dma((n,)), dma((n,)), dma((n,)),
        ],
        compiler_params=pltpu.CompilerParams(collective_id=1, has_side_effects=True),
        name="reduce",
    )(qkv, out, fc1, fc2, bias, gm, ada)


def per_device(
    n, c,
    tokens, condition,
    ada_weight, ada_bias, qkv_weight, qv_bias, out_weight, out_bias,
    fc1_weight, fc1_bias, fc2_weight, fc2_bias,
    cotangent,
):
    latents, local_rows, width = tokens.shape
    me, row = lax.axis_index("fsdp"), lax.axis_index("ctx")
    scale_factor = HEAD ** (-0.5)
    tok = tokens[0]
    slice_rows = ada_weight.shape[0]
    cond_float = condition.astype(F32)
    cond_silu = jax.nn.silu(cond_float).astype(BF16)
    cond_columns = jnp.broadcast_to(
        cond_silu.astype(F32).reshape(n, slice_rows, 1), (n, slice_rows, 128)
    )
    bias_row = lax.dynamic_update_slice(
        jnp.zeros((1, ada_bias.shape[0] * n), F32),
        ada_bias.astype(F32)[None, :],
        (0, me * ada_bias.shape[0]),
    )
    biases = jnp.concatenate([qv_bias, out_bias, fc1_bias, fc2_bias]).astype(F32)
    small = jnp.pad(biases, (0, 256 - biases.shape[0]))[None, :]
    qkv_all, out_all, fc1_all, fc2_all, tok_all, cond_all, modulation, small_all = gather(
        n, c, qkv_weight, out_weight, fc1_weight, fc2_weight, tok, cond_columns,
        ada_weight, bias_row, small,
    )
    qkv_full = qkv_all.reshape(-1, qkv_weight.shape[1])
    out_full = out_all.reshape(-1, width)
    fc1_full = fc1_all.reshape(-1, fc1_weight.shape[1])
    fc2_full = fc2_all.reshape(-1, width)
    pieces, start = [], 0
    for piece in (qv_bias, out_bias, fc1_bias, fc2_bias):
        pieces.append(small_all[:, 0, start : start + piece.shape[0]].reshape(1, -1))
        start += piece.shape[0]
    qv_full, out_bias_full, fc1_bias_full, fc2_bias_full = pieces
    shift_one, scale_one, gate_one, shift_two, scale_two, gate_two = jnp.split(
        modulation, 6, axis=1
    )
    order = [lax.rem(row + k, c) for k in range(c)]
    rotated = jnp.concatenate([tok] + [tok_all[i] for i in order[1:]], axis=0)
    residual_all = rotated.astype(F32)
    normed_all, inverse_all = layer_stats(residual_all)
    hidden_all = (normed_all * (1.0 + scale_one) + shift_one).astype(BF16)
    residual = residual_all[:local_rows]
    normed_one, inverse_one = normed_all[:local_rows], inverse_all[:local_rows]
    hidden_one = hidden_all[:local_rows]
    queries = (matmul(hidden_one, qkv_full[:, :width]) + qv_full[:, :width]).astype(BF16)
    keys = matmul(hidden_all, qkv_full[:, width : 2 * width]).astype(BF16)
    values = (matmul(hidden_all, qkv_full[:, 2 * width :]) + qv_full[:, width:]).astype(BF16)

    def head(array, h):
        return array[:, h * HEAD : (h + 1) * HEAD]

    probabilities, mixed_heads = [], []
    for h in range(HEADS):
        scores = matmul_nt(head(queries, h), head(keys, h)) * scale_factor
        raised = jnp.exp(scores - jnp.max(scores, axis=1, keepdims=True))
        probability = raised / jnp.sum(raised, axis=1, keepdims=True)
        probabilities.append(probability)
        mixed_heads.append(matmul(probability.astype(BF16), head(values, h)))
    mixed = jnp.concatenate(mixed_heads, axis=1).astype(BF16)
    attn_out = matmul(mixed, out_full) + out_bias_full
    after_attn = residual + gate_one * attn_out
    normed_two, inverse_two = layer_stats(after_attn)
    hidden_two = (normed_two * (1.0 + scale_two) + shift_two).astype(BF16)
    pre_act = matmul(hidden_two, fc1_full) + fc1_bias_full
    activated = jax.nn.gelu(pre_act, approximate=True).astype(BF16)
    mlp_out = matmul(activated, fc2_full) + fc2_bias_full
    result = (after_attn + gate_two * mlp_out).astype(BF16)

    grad_result = cotangent[0].astype(F32)
    grad_gate_two = jnp.sum(grad_result * mlp_out, axis=0, keepdims=True)
    grad_mlp_float = grad_result * gate_two
    grad_mlp = grad_mlp_float.astype(BF16)
    grad_fc2_w = matmul_tn(activated, grad_mlp)
    grad_fc2_b = jnp.sum(grad_mlp_float, axis=0)
    grad_pre = gelu_back(pre_act, matmul_nt(grad_mlp, fc2_full))
    grad_pre_half = grad_pre.astype(BF16)
    grad_fc1_w = matmul_tn(hidden_two, grad_pre_half)
    grad_fc1_b = jnp.sum(grad_pre, axis=0)
    grad_hidden_two = matmul_nt(grad_pre_half, fc1_full)
    grad_scale_two = jnp.sum(grad_hidden_two * normed_two, axis=0, keepdims=True)
    grad_shift_two = jnp.sum(grad_hidden_two, axis=0, keepdims=True)
    grad_after = grad_result + layer_back(
        normed_two, inverse_two, grad_hidden_two * (1.0 + scale_two)
    )
    grad_gate_one = jnp.sum(grad_after * attn_out, axis=0, keepdims=True)
    grad_attn_float = grad_after * gate_one
    grad_attn = grad_attn_float.astype(BF16)
    grad_out_w = matmul_tn(mixed, grad_attn)
    grad_out_b = jnp.sum(grad_attn_float, axis=0)
    grad_mixed = matmul_nt(grad_attn, out_full).astype(BF16)
    grad_q, grad_k, grad_v = [], [], []
    for h in range(HEADS):
        grad_head = head(grad_mixed, h)
        inner = jnp.sum(
            grad_head.astype(F32) * head(mixed, h).astype(F32), axis=1, keepdims=True
        )
        grad_prob = matmul_nt(grad_head, head(values, h))
        grad_scores = (probabilities[h] * (grad_prob - inner) * scale_factor).astype(BF16)
        grad_q.append(matmul(grad_scores, head(keys, h)))
        grad_k.append(matmul_tn(grad_scores, head(queries, h)))
        grad_v.append(matmul_tn(probabilities[h].astype(BF16), grad_head))
    grad_query = jnp.concatenate(grad_q, axis=1)
    grad_value = jnp.concatenate(grad_v, axis=1)
    grad_qv_b = jnp.concatenate([jnp.sum(grad_query, axis=0), jnp.sum(grad_value, axis=0)])
    grad_kv = jnp.concatenate(grad_k + grad_v, axis=1).astype(BF16)
    grad_query = grad_query.astype(BF16)
    grad_hidden_kv = matmul_nt(grad_kv, qkv_full[:, width:])
    grad_hidden_one = grad_hidden_kv[:local_rows] + matmul_nt(grad_query, qkv_full[:, :width])
    for k in range(1, c):
        sent = grad_hidden_kv[k * local_rows : (k + 1) * local_rows].astype(BF16)
        moved = lax.ppermute(sent, "ctx", [(i, (i + k) % c) for i in range(c)])
        grad_hidden_one = grad_hidden_one + moved.astype(F32)
    grad_qkv_w = jnp.concatenate(
        [matmul_tn(hidden_one, grad_query), matmul_tn(hidden_all, grad_kv)], axis=1
    )
    grad_scale_one = jnp.sum(grad_hidden_one * normed_one, axis=0, keepdims=True)
    grad_shift_one = jnp.sum(grad_hidden_one, axis=0, keepdims=True)
    grad_input = (
        grad_after + layer_back(normed_one, inverse_one, grad_hidden_one * (1.0 + scale_one))
    ).astype(BF16)
    grad_mod = jnp.concatenate(
        [grad_shift_one, grad_scale_one, grad_gate_one, grad_shift_two, grad_scale_two,
         grad_gate_two],
        axis=1,
    )
    bias_grads = jnp.concatenate(
        [g.reshape(n, -1) for g in (grad_qv_b, grad_out_b, grad_fc1_b, grad_fc2_b)], axis=1
    )
    bias_grads = jnp.pad(bias_grads, ((0, 0), (0, 1024 - bias_grads.shape[1])))
    ada_rows = jnp.pad(ada_weight.astype(F32), ((0, 128 - slice_rows), (0, 0)))
    qkv_sum, out_sum, fc1_sum, fc2_sum, bias_sum, mod_all, back_all = reduce(
        n, c,
        grad_qkv_w.astype(BF16).reshape(qkv_all.shape),
        grad_out_w.astype(BF16).reshape(out_all.shape),
        grad_fc1_w.astype(BF16).reshape(fc1_all.shape),
        grad_fc2_w.astype(BF16).reshape(fc2_all.shape),
        bias_grads.reshape(n, 8, 128), grad_mod, ada_rows,
    )
    mod_all = mod_all[:, 0, :]
    grad_ada_w = lax.dot_general(
        cond_all[:, :, 0], mod_all, (((0,), (0,)), ((), ())),
        precision=lax.Precision.HIGHEST, preferred_element_type=F32,
    )
    grad_ada_b = jnp.sum(
        lax.dynamic_slice(mod_all, (0, me * ada_bias.shape[0]), (n, ada_bias.shape[0])), axis=0
    )
    ada_back_term = back_all[:, 0, :slice_rows].reshape(1, -1)
    grad_cond = jax.vjp(jax.nn.silu, cond_float)[1](ada_back_term)[0]
    flat, parts, start = bias_sum.reshape(-1), [], 0
    for piece in (qv_bias, out_bias, fc1_bias, fc2_bias):
        parts.append(flat[start : start + piece.shape[0]])
        start += piece.shape[0]
    return (
        result[None], grad_input[None], grad_cond,
        grad_ada_w, grad_ada_b,
        qkv_sum, parts[0], out_sum, parts[1], fc1_sum, parts[2], fc2_sum, parts[3],
    )


def solution(mesh):
    n, c = mesh.shape["fsdp"], mesh.shape["ctx"]
    return jax.shard_map(
        partial(per_device, n, c),
        mesh=mesh,
        in_specs=(
            P("fsdp", "ctx", None),
            P("fsdp", None),
            P("fsdp", None),
            P("fsdp"),
            P("fsdp", None),
            P("fsdp"),
            P("fsdp", None),
            P("fsdp"),
            P("fsdp", None),
            P("fsdp"),
            P("fsdp", None),
            P("fsdp"),
            P("fsdp", "ctx", None),
        ),
        out_specs=(
            P("fsdp", "ctx", None),
            P("fsdp", "ctx", None),
            P("fsdp", None),
            P("fsdp", None),
            P("fsdp"),
            P("fsdp", None),
            P("fsdp"),
            P("fsdp", None),
            P("fsdp"),
            P("fsdp", None),
            P("fsdp"),
            P("fsdp", None),
            P("fsdp"),
        ),
        check_vma=False,
    )
```

```python
from functools import partial

import jax
import jax.numpy as jnp
from jax import lax
from jax.experimental import pallas as pl
from jax.experimental.pallas import tpu as pltpu
from jax.sharding import PartitionSpec as P

HEADS = 6
HEAD = 64
MESH = pl.DeviceIdType.MESH
F32 = jnp.float32
BF16 = jnp.bfloat16


epsilon = 1e-06


def layer_stats(values):
    centered = values - jnp.mean(values, axis=-1, keepdims=True)
    inverse = lax.rsqrt(jnp.mean(centered * centered, axis=-1, keepdims=True) + epsilon)
    return (centered * inverse, inverse)


def layer_back(normed, inverse, grad_normed):
    mean_grad = jnp.mean(grad_normed, axis=-1, keepdims=True)
    mean_prod = jnp.mean(grad_normed * normed, axis=-1, keepdims=True)
    return inverse * (grad_normed - mean_grad - normed * mean_prod)


def gelu_pair(hidden):
    root = (2.0 / 3.141592653589793) ** 0.5
    square = hidden * hidden
    curve = jnp.tanh(root * (hidden + 0.044715 * square * hidden))
    cdf = 0.5 * (1.0 + curve)
    slope = cdf + 0.5 * hidden * (1.0 - curve * curve) * root * (1.0 + 3 * 0.044715 * square)
    return (hidden * cdf, slope)


def matmul(left, right):
    return jnp.dot(left, right, preferred_element_type=F32)


def matmul_nt(left, right):
    return lax.dot_general(left, right, (((1,), (1,)), ((), ())), preferred_element_type=F32)


def matmul_tn(left, right):
    return lax.dot_general(left, right, (((0,), (0,)), ((), ())), preferred_element_type=F32)


def flip(index, mask):
    return index + mask - 2 * mask * ((index // mask) % 2)


def loop(count, body):
    def step(i, carry):
        body(i)
        return carry

    lax.fori_loop(0, count, step, 0)


def remote(src, dst, send, recv, **device):
    return pltpu.make_async_remote_copy(
        src_ref=src, dst_ref=dst, send_sem=send, recv_sem=recv,
        device_id=device, device_id_type=MESH,
    )


def meet(n, c, me, row):
    barrier = pltpu.get_barrier_semaphore()

    def greet_fsdp(k):
        pl.semaphore_signal(
            barrier, inc=1, device_id={"fsdp": (me + 1 + k) % n}, device_id_type=MESH
        )

    def greet_ctx(k):
        pl.semaphore_signal(
            barrier, inc=1, device_id={"ctx": (row + 1 + k) % c}, device_id_type=MESH
        )

    loop(n - 1, greet_fsdp)
    loop(c - 1, greet_ctx)
    pl.semaphore_wait(barrier, n + c - 2)


def gather_kernel(
    n, c,
    qkv, out, fc1, fc2, tok, cond, ada, ada_bias, small,
    qkv_all, out_all, fc1_all, fc2_all, tok_all, cond_out, mod, small_all,
    cond_all, part, mod_all,
    send_w, recv_w, send_t, recv_t, send_c, recv_c, send_m, recv_m, send_s, recv_s,
):
    me, row = lax.axis_index("fsdp"), lax.axis_index("ctx")
    own = (qkv, out, fc1, fc2)
    full = (qkv_all, out_all, fc1_all, fc2_all)
    stages = n.bit_length() - 1
    meet(n, c, me, row)

    def cond_copy(to, sender):
        return remote(
            cond.at[to], cond_all.at[sender], send_c.at[to], recv_c.at[sender], fsdp=to
        )

    def small_copy(to, sender):
        return remote(small, small_all.at[sender], send_s.at[to], recv_s.at[sender], fsdp=to)

    def mod_copy(to, sender):
        return remote(part.at[to], mod_all.at[sender], send_m.at[to], recv_m.at[sender], fsdp=to)

    def tok_copy(to, sender):
        return remote(tok, tok_all.at[sender], send_t.at[to], recv_t.at[sender], ctx=to)

    def weight_copy(w, s, block, mine):
        return remote(
            own[w] if mine else full[w].at[block],
            full[w].at[block],
            send_w.at[w, s, block],
            recv_w.at[w, block],
            fsdp=flip(me, n >> (s + 1)),
        )

    def others(body):
        loop(n - 1, lambda k: body((me + 1 + k) % n))

    def siblings(body):
        loop(c - 1, lambda k: body((row + 1 + k) % c))

    relay = stages - 2 if c == 2 and stages >= 3 else -1

    def relay_copy(w, block):
        return remote(
            full[w].at[block], full[w].at[block],
            send_w.at[w, stages, block], recv_w.at[w, block], ctx=(row + 1) % c,
        )

    def forward(w, s, block, mine):
        if s != relay:
            weight_copy(w, s, block, mine).start()
            return

        @pl.when((block // (2 * (n >> (s + 1)))) % 2 == row)
        def _():
            weight_copy(w, s, block, mine).start()

    others(lambda to: cond_copy(to, me).start())
    for w in range(4):
        for s in range(stages):
            forward(w, s, me, True)
    others(lambda to: small_copy(to, me).start())
    siblings(lambda to: tok_copy(to, row).start())
    for w in range(4):
        full[w][me] = own[w][...]
    tok_all[row] = tok[...]
    small_all[me] = small[...]
    cond_all[me] = cond[me]
    others(lambda peer: cond_copy(peer, peer).wait_recv())
    lane = lax.broadcasted_iota(jnp.int32, cond_all.shape[1:], 1)
    columns = jnp.zeros(cond_all.shape[1:], F32)
    for i in range(n):
        columns = jnp.where(lane == i, cond_all[i], columns)
    cond_out[...] = columns
    partial_mod = matmul_tn(columns.astype(BF16), ada[...])
    for i in range(n):
        part[i] = partial_mod[i : i + 1, :] + ada_bias[...]
    others(lambda to: mod_copy(to, me).start())
    mod_all[me] = part[me]

    for s in range(stages):
        mask = n >> (s + 1)
        origin = flip(me, mask) % (2 * mask)

        def arrived(t, s=s, mask=mask, origin=origin, across=False):
            block = origin + t * (2 * mask)
            for w in range(4):
                weight_copy(w, s, block, False).wait_recv()
                if across:
                    relay_copy(w, block).start()
                for later in range(s + 1, stages):
                    forward(w, later, block, False)

        if s == relay:
            loop(1 << (s - 1), lambda t: arrived(2 * t + row, across=True))
            loop(1 << (s - 1), lambda t: arrived(2 * t + 1 - row))
        else:
            loop(1 << s, arrived)

    others(lambda peer: mod_copy(peer, peer).wait_recv())
    total = mod_all[0]
    for i in range(1, n):
        total = total + mod_all[i]
    mod[...] = total
    others(lambda peer: small_copy(peer, peer).wait_recv())
    siblings(lambda peer: tok_copy(peer, peer).wait_recv())
    for s in range(stages):
        mask = n >> (s + 1)

        def left(t, s=s, mask=mask):
            block = me % (2 * mask) + t * (2 * mask)
            for w in range(4):
                weight_copy(w, s, block, False).wait_send()

        def crossed(t, mask=mask):
            block = flip(me, mask) % (2 * mask) + t * (2 * mask)
            for w in range(4):
                relay_copy(w, block).wait_send()

        if s == relay:
            loop(1 << (s - 1), lambda t: left(2 * t + row))
            loop(1 << (s - 1), lambda t: crossed(2 * t + row))
        else:
            loop(1 << s, left)
    others(lambda to: cond_copy(to, me).wait_send())
    others(lambda to: small_copy(to, me).wait_send())
    others(lambda to: mod_copy(to, me).wait_send())
    siblings(lambda to: tok_copy(to, row).wait_send())


def vmem(count):
    return [pl.BlockSpec(memory_space=pltpu.VMEM)] * count


def gather(n, c, qkv, out, fc1, fc2, tok, cond, ada, ada_bias, small):
    stages = n.bit_length() - 1
    shape = jax.ShapeDtypeStruct
    dma = pltpu.SemaphoreType.DMA
    return pl.pallas_call(
        partial(gather_kernel, n, c),
        out_shape=[shape((n, *w.shape), BF16) for w in (qkv, out, fc1, fc2)]
        + [
            shape((c, *tok.shape), BF16),
            shape(cond.shape[1:], F32),
            shape(ada_bias.shape, F32),
            shape((n, *small.shape), F32),
        ],
        in_specs=vmem(9),
        out_specs=vmem(8),
        scratch_shapes=[
            pltpu.VMEM(cond.shape, F32),
            pltpu.VMEM((n, *ada_bias.shape), F32),
            pltpu.VMEM((n, *ada_bias.shape), F32),
            dma((4, stages + 1, n)), dma((4, n)),
            dma((c,)), dma((c,)), dma((n,)), dma((n,)), dma((n,)), dma((n,)), dma((n,)), dma((n,)),
        ],
        compiler_params=pltpu.CompilerParams(collective_id=0, has_side_effects=True),
        name="gather",
    )(qkv, out, fc1, fc2, tok, cond, ada, ada_bias, small)


def reduce_kernel(
    n, c,
    qkv, out, fc1, fc2, line, ada, columns, tok, mod, after, hid_own, hid_sent,
    qkv_sum, out_sum, fc1_sum, fc2_sum, grad_input, grad_ada, total_line, back_all,
    *scratch,
):
    stages = n.bit_length() - 1
    me, row = lax.axis_index("fsdp"), lax.axis_index("ctx")
    given = (qkv, out, fc1, fc2)
    sums = (qkv_sum, out_sum, fc1_sum, fc2_sum)
    arrays = len(given)
    incoming = [scratch[w * stages : (w + 1) * stages] for w in range(arrays)]
    scratch = scratch[arrays * stages :]
    kept = [scratch[w * stages : (w + 1) * stages] for w in range(arrays)]
    scratch = scratch[arrays * stages :]
    shares, scratch = scratch[:arrays], scratch[arrays:]
    (gm, gm_ctx, gm_mine, gm_all, back, hid, send_r, recv_r, send_x, recv_x, send_g, recv_g,
     send_f, recv_f, send_b, recv_b, send_h, recv_h) = scratch
    width = tok.shape[1]
    meet(n, c, me, row)

    def others(body):
        loop(n - 1, lambda k: body((me + 1 + k) % n))

    def siblings(body):
        loop(c - 1, lambda k: body((row + 1 + k) % c))

    def ctx_gm(to, sender):
        return remote(gm, gm_ctx.at[sender], send_g.at[to], recv_g.at[sender], ctx=to)

    def fsdp_gm(to, sender):
        return remote(gm_mine, gm_all.at[sender], send_f.at[to], recv_f.at[sender], fsdp=to)

    def back_copy(to, sender):
        return remote(back.at[to], back_all.at[sender], send_b.at[to], recv_b.at[sender], fsdp=to)

    def share_copy(w, to, sender):
        return remote(
            shares[w].at[row], shares[w].at[sender], send_x.at[w, to], recv_x.at[w, sender], ctx=to
        )

    def bit(s):
        return (me // (1 << s)) % 2

    def source(w, s):
        return given[w] if s == 0 else kept[w][s - 1]

    def halve(w, s, j):
        return remote(
            source(w, s).at[2 * j + 1 - bit(s)],
            incoming[w][s].at[j],
            send_r.at[w, s, j],
            recv_r.at[w, s, j],
            fsdp=flip(me, 1 << s),
        )

    def hid_copy(k):
        return remote(
            hid_sent.at[k], hid.at[k], send_h.at[k], recv_h.at[k], ctx=(row + 1 + k) % c
        )

    for k in range(c - 1):
        hid_copy(k).start()

    def send_all(s, base, step, count):
        def body(t):
            for w in range(arrays):
                halve(w, s, base + step * t).start()

        loop(count, body)

    send_all(0, 1 - bit(1), 2, n // 4)
    send_all(0, bit(1), 2, n // 4)

    normed, inverse = layer_stats(tok[...].astype(F32))
    grad_hidden = hid_own[...]
    for k in range(c - 1):
        hid_copy(k).wait_recv()
        grad_hidden = grad_hidden + hid[k].astype(F32)
    grad_input[...] = (
        after[...]
        + layer_back(normed, inverse, grad_hidden * (1.0 + mod[:, width : 2 * width]))
    ).astype(BF16)
    gm[:, :width] = jnp.sum(grad_hidden, axis=0, keepdims=True)
    gm[:, width : 2 * width] = jnp.sum(grad_hidden * normed, axis=0, keepdims=True)
    gm[:, 2 * width :] = line[:, 2 * width :]
    siblings(lambda to: ctx_gm(to, row).start())
    gm_ctx[row] = gm[...]
    siblings(lambda peer: ctx_gm(peer, peer).wait_recv())
    total = gm_ctx[0]
    for i in range(1, c):
        total = total + gm_ctx[i]
    gm_mine[...] = total
    gm_all[me] = total
    others(lambda to: fsdp_gm(to, me).start())

    def backward():
        others(lambda peer: fsdp_gm(peer, peer).wait_recv())
        rows = lax.broadcasted_iota(jnp.int32, (n, gm.shape[1]), 0)
        stacked = jnp.zeros((n, gm.shape[1]), F32)
        for i in range(n):
            stacked = jnp.where(rows == i, jnp.broadcast_to(gm_all[i], stacked.shape), stacked)
        wide = 6 * width
        total_line[...] = jnp.sum(stacked, axis=0, keepdims=True)
        grad_ada[...] = lax.dot_general(
            columns[...][:, :n], stacked[:, :wide], (((1,), (0,)), ((), ())),
            preferred_element_type=F32, precision=lax.Precision.HIGHEST,
        )
        product = lax.dot_general(
            stacked[:, :wide], ada[...], (((1,), (1,)), ((), ())),
            preferred_element_type=F32, precision=lax.Precision.HIGHEST,
        )
        for i in range(n):
            back[i] = product[i : i + 1, :]
        others(lambda to: back_copy(to, me).start())
        back_all[me] = back[me]

    def add(w, s, j):
        halve(w, s, j).wait_recv()
        value = source(w, s)[2 * j + bit(s)].astype(F32) + incoming[w][s][j].astype(F32)
        if s == stages - 1:
            shares[w][row] = value.astype(given[w].dtype)
        else:
            kept[w][s][j] = value.astype(given[w].dtype)

    for s in range(stages):
        if s == stages - 1:
            for w in range(arrays):
                add(w, s, 0)
                siblings(lambda to, w=w: share_copy(w, to, row).start())
            continue

        def first(t, s=s):
            j = 2 * t + 1 - bit(s + 1)
            for w in range(arrays):
                add(w, s, j)
                halve(w, s + 1, t).start()

        def second(t, s=s):
            for w in range(arrays):
                add(w, s, 2 * t + bit(s + 1))

        loop(n >> (s + 2), first)
        loop(n >> (s + 2), second)
        if s == 0:
            backward()

    for w in range(arrays):
        siblings(lambda peer, w=w: share_copy(w, peer, peer).wait_recv())
        value = shares[w][0].astype(F32)
        for i in range(1, c):
            value = value + shares[w][i].astype(F32)
        sums[w][...] = value
    others(lambda peer: back_copy(peer, peer).wait_recv())

    for k in range(c - 1):
        hid_copy(k).wait_send()
    siblings(lambda to: ctx_gm(to, row).wait_send())
    others(lambda to: fsdp_gm(to, me).wait_send())
    others(lambda to: back_copy(to, me).wait_send())
    for s in range(stages):

        def sent(j, s=s):
            for w in range(arrays):
                halve(w, s, j).wait_send()

        loop(n >> (s + 1), sent)
    for w in range(arrays):
        siblings(lambda to, w=w: share_copy(w, to, row).wait_send())


def reduce(n, c, qkv, out, fc1, fc2, line, ada, columns, tok, mod, after, hid_own, hid_sent):
    stages = n.bit_length() - 1
    shape = jax.ShapeDtypeStruct
    dma = pltpu.SemaphoreType.DMA
    given = (qkv, out, fc1, fc2)
    halves = [
        pltpu.VMEM((n >> (s + 1), *w.shape[1:]), w.dtype) for w in given for s in range(stages)
    ]
    back = (n, 1, ada.shape[0])
    return pl.pallas_call(
        partial(reduce_kernel, n, c),
        out_shape=[shape(w.shape[1:], F32) for w in given]
        + [
            shape(tok.shape, BF16),
            shape((columns.shape[0], mod.shape[1]), F32),
            shape(line.shape, F32),
            shape(back, F32),
        ],
        in_specs=vmem(12),
        out_specs=vmem(8),
        scratch_shapes=halves
        + halves
        + [pltpu.VMEM((c, *w.shape[1:]), w.dtype) for w in given]
        + [
            pltpu.VMEM(line.shape, F32),
            pltpu.VMEM((c, *line.shape), F32),
            pltpu.VMEM(line.shape, F32),
            pltpu.VMEM((n, *line.shape), F32),
            pltpu.VMEM(back, F32),
            pltpu.VMEM(hid_sent.shape, BF16),
            dma((4, stages, n // 2)), dma((4, stages, n // 2)),
            dma((4, c)), dma((4, c)), dma((c,)), dma((c,)),
            dma((n,)), dma((n,)), dma((n,)), dma((n,)), dma((c,)), dma((c,)),
        ],
        compiler_params=pltpu.CompilerParams(collective_id=1, has_side_effects=True),
        name="reduce",
    )(qkv, out, fc1, fc2, line, ada, columns, tok, mod, after, hid_own, hid_sent)


def head(array, h):
    return array[:, h * HEAD : (h + 1) * HEAD]


def block_kernel(
    c,
    qkv_ref, out_ref, fc1_ref, fc2_ref, tok_ref, mod_ref, bias_ref, cot_ref,
    result_ref, after_ref, hid_own_ref, hid_sent_ref, qkv_grad, out_grad, fc1_grad, fc2_grad,
    line_ref,
):
    width = cot_ref.shape[1]
    rows = cot_ref.shape[0]
    hidden_width = fc1_ref.shape[1]
    scale_factor = HEAD ** (-0.5)
    shift_one, scale_one, gate_one, shift_two, scale_two, gate_two = (
        mod_ref[:, k * width : (k + 1) * width] for k in range(6)
    )
    starts = (0, width, 2 * width, 3 * width, 3 * width + hidden_width, 4 * width + hidden_width)
    query_bias, value_bias, out_bias, fc1_bias, fc2_bias = (
        bias_ref[:, a:b] for a, b in zip(starts, starts[1:])
    )
    residual_all = tok_ref[...].astype(F32)
    normed_all, _ = layer_stats(residual_all)
    hidden_all = (normed_all * (1.0 + scale_one) + shift_one).astype(BF16)
    residual, hidden_one = residual_all[:rows], hidden_all[:rows]
    queries = (matmul(hidden_one, qkv_ref[:, :width]) + query_bias).astype(BF16)
    keys = matmul(hidden_all, qkv_ref[:, width : 2 * width]).astype(BF16)
    values = (matmul(hidden_all, qkv_ref[:, 2 * width :]) + value_bias).astype(BF16)
    probabilities, mixed_heads = [], []
    for h in range(HEADS):
        scores = matmul_nt(head(queries, h), head(keys, h)) * scale_factor
        raised = jnp.exp(scores - jnp.max(scores, axis=1, keepdims=True))
        probability = raised * (1.0 / jnp.sum(raised, axis=1, keepdims=True))
        probabilities.append(probability)
        mixed_heads.append(matmul(probability.astype(BF16), head(values, h)))
    mixed = jnp.concatenate(mixed_heads, axis=1).astype(BF16)
    attn_out = matmul(mixed, out_ref[...]) + out_bias
    after_attn = residual + gate_one * attn_out
    normed_two, inverse_two = layer_stats(after_attn)
    hidden_two = (normed_two * (1.0 + scale_two) + shift_two).astype(BF16)
    pre_act = matmul(hidden_two, fc1_ref[...]) + fc1_bias
    activated, slope = gelu_pair(pre_act)
    activated = activated.astype(BF16)
    mlp_out = matmul(activated, fc2_ref[...]) + fc2_bias
    result_ref[...] = (after_attn + gate_two * mlp_out).astype(BF16)

    def total(array):
        return jnp.sum(array, axis=0, keepdims=True)

    grad_result = cot_ref[...].astype(F32)
    grad_mlp_float = grad_result * gate_two
    grad_mlp = grad_mlp_float.astype(BF16)
    fc2_grad[...] = matmul_tn(activated, grad_mlp).astype(BF16)
    grad_pre = slope * matmul_nt(grad_mlp, fc2_ref[...])
    grad_pre_half = grad_pre.astype(BF16)
    fc1_grad[...] = matmul_tn(hidden_two, grad_pre_half).astype(BF16)
    grad_hidden_two = matmul_nt(grad_pre_half, fc1_ref[...])
    grad_after = grad_result + layer_back(
        normed_two, inverse_two, grad_hidden_two * (1.0 + scale_two)
    )
    after_ref[...] = grad_after
    grad_attn_float = grad_after * gate_one
    grad_attn = grad_attn_float.astype(BF16)
    out_grad[...] = matmul_tn(mixed, grad_attn).astype(BF16)
    grad_mixed = matmul_nt(grad_attn, out_ref[...]).astype(BF16)
    grad_q, grad_k, grad_v = [], [], []
    for h in range(HEADS):
        grad_head = head(grad_mixed, h)
        inner = jnp.sum(
            grad_head.astype(F32) * head(mixed, h).astype(F32), axis=1, keepdims=True
        )
        grad_prob = matmul_nt(grad_head, head(values, h))
        grad_scores = (probabilities[h] * (grad_prob - inner) * scale_factor).astype(BF16)
        grad_q.append(matmul(grad_scores, head(keys, h)))
        grad_k.append(matmul_tn(grad_scores, head(queries, h)))
        grad_v.append(matmul_tn(probabilities[h].astype(BF16), grad_head))
    grad_query = jnp.concatenate(grad_q, axis=1)
    grad_value = jnp.concatenate(grad_v, axis=1)
    grad_kv = jnp.concatenate(grad_k + grad_v, axis=1).astype(BF16)
    query_half = grad_query.astype(BF16)
    hid_kv = matmul_nt(grad_kv, qkv_ref[:, width:])
    hid_own_ref[...] = hid_kv[:rows] + matmul_nt(query_half, qkv_ref[:, :width])
    for k in range(1, c):
        hid_sent_ref[k - 1] = hid_kv[k * rows : (k + 1) * rows].astype(BF16)
    qkv_grad[:, :width] = matmul_tn(hidden_one, query_half).astype(BF16)
    qkv_grad[:, width:] = matmul_tn(hidden_all, grad_kv).astype(BF16)
    line = (
        jnp.zeros((1, 2 * width), F32),
        total(grad_after * attn_out),
        total(grad_hidden_two),
        total(grad_hidden_two * normed_two),
        total(grad_result * mlp_out),
        total(grad_query),
        total(grad_value),
        total(grad_attn_float),
        total(grad_pre),
        total(grad_mlp_float),
    )
    start = 0
    for piece in line:
        line_ref[:, start : start + piece.shape[1]] = piece
        start += piece.shape[1]


def block(c, qkv, out, fc1, fc2, tok, mod, bias, cot):
    shape = jax.ShapeDtypeStruct
    return pl.pallas_call(
        partial(block_kernel, c),
        out_shape=[
            shape(cot.shape, BF16),
            shape(cot.shape, F32),
            shape(cot.shape, F32),
            shape((c - 1, *cot.shape), BF16),
            shape(qkv.shape, BF16),
            shape(out.shape, BF16),
            shape(fc1.shape, BF16),
            shape(fc2.shape, BF16),
            shape((1, mod.shape[1] + bias.shape[1]), F32),
        ],
        in_specs=vmem(8),
        out_specs=vmem(9),
        name="block",
    )(qkv, out, fc1, fc2, tok, mod, bias, cot)


def per_device(
    n, c,
    tokens, condition,
    ada_weight, ada_bias, qkv_weight, qv_bias, out_weight, out_bias,
    fc1_weight, fc1_bias, fc2_weight, fc2_bias,
    cotangent,
):
    latents, local_rows, width = tokens.shape
    me, row = lax.axis_index("fsdp"), lax.axis_index("ctx")
    scale_factor = HEAD ** (-0.5)
    tok = tokens[0]
    slice_rows = ada_weight.shape[0]
    cond_float = condition.astype(F32)
    cond_silu = jax.nn.silu(cond_float).astype(BF16)
    cond_columns = jnp.broadcast_to(
        cond_silu.astype(F32).reshape(n, slice_rows, 1), (n, slice_rows, 128)
    )
    bias_row = lax.dynamic_update_slice(
        jnp.zeros((1, ada_bias.shape[0] * n), F32),
        ada_bias.astype(F32)[None, :],
        (0, me * ada_bias.shape[0]),
    )
    biases = jnp.concatenate([qv_bias, out_bias, fc1_bias, fc2_bias]).astype(F32)
    small = jnp.pad(biases, (0, 256 - biases.shape[0]))[None, :]
    qkv_all, out_all, fc1_all, fc2_all, tok_all, columns, modulation, small_all = gather(
        n, c, qkv_weight, out_weight, fc1_weight, fc2_weight, tok, cond_columns,
        ada_weight, bias_row, small,
    )
    pieces, start = [], 0
    for piece in (qv_bias, out_bias, fc1_bias, fc2_bias):
        pieces.append(small_all[:, 0, start : start + piece.shape[0]].reshape(1, -1))
        start += piece.shape[0]
    order = [lax.rem(row + k, c) for k in range(c)]
    rotated = jnp.concatenate([tok] + [tok_all[i] for i in order[1:]], axis=0)
    result, after, hid_own, hid_sent, grad_qkv, grad_out, grad_fc1, grad_fc2, line = block(
        c,
        qkv_all.reshape(-1, qkv_weight.shape[1]),
        out_all.reshape(-1, width),
        fc1_all.reshape(-1, fc1_weight.shape[1]),
        fc2_all.reshape(-1, width),
        rotated, modulation, jnp.concatenate(pieces, axis=1), cotangent[0],
    )
    ada_rows = jnp.pad(ada_weight.astype(F32), ((0, 128 - slice_rows), (0, 0)))
    qkv_sum, out_sum, fc1_sum, fc2_sum, grad_input, grad_ada_w, total_line, back_all = reduce(
        n, c,
        grad_qkv.reshape(qkv_all.shape),
        grad_out.reshape(out_all.shape),
        grad_fc1.reshape(fc1_all.shape),
        grad_fc2.reshape(fc2_all.shape),
        line, ada_rows, columns, tok, modulation, after, hid_own, hid_sent,
    )
    ada_back_term = back_all[:, 0, :slice_rows].reshape(1, -1)
    grad_cond = jax.vjp(jax.nn.silu, cond_float)[1](ada_back_term)[0]
    parts, start = [], 0
    for piece in (ada_bias, qv_bias, out_bias, fc1_bias, fc2_bias):
        size = piece.shape[0]
        parts.append(lax.dynamic_slice(total_line, (0, start + me * size), (1, size))[0])
        start += n * size
    return (
        result[None], grad_input[None], grad_cond,
        grad_ada_w, parts[0],
        qkv_sum, parts[1], out_sum, parts[2], fc1_sum, parts[3], fc2_sum, parts[4],
    )


def solution(mesh):
    n, c = mesh.shape["fsdp"], mesh.shape["ctx"]
    return jax.shard_map(
        partial(per_device, n, c),
        mesh=mesh,
        in_specs=(
            P("fsdp", "ctx", None),
            P("fsdp", None),
            P("fsdp", None),
            P("fsdp"),
            P("fsdp", None),
            P("fsdp"),
            P("fsdp", None),
            P("fsdp"),
            P("fsdp", None),
            P("fsdp"),
            P("fsdp", None),
            P("fsdp"),
            P("fsdp", "ctx", None),
        ),
        out_specs=(
            P("fsdp", "ctx", None),
            P("fsdp", "ctx", None),
            P("fsdp", None),
            P("fsdp", None),
            P("fsdp"),
            P("fsdp", None),
            P("fsdp"),
            P("fsdp", None),
            P("fsdp"),
            P("fsdp", None),
            P("fsdp"),
            P("fsdp", None),
            P("fsdp"),
        ),
        check_vma=False,
    )
```

```python
from functools import partial

import jax
import jax.numpy as jnp
from jax import lax
from jax.experimental import pallas as pl
from jax.experimental.pallas import tpu as pltpu
from jax.sharding import PartitionSpec as P

HEADS = 6
HEAD = 64
MESH = pl.DeviceIdType.MESH
F32 = jnp.float32
BF16 = jnp.bfloat16


epsilon = 1e-06


def layer_stats(values):
    centered = values - jnp.mean(values, axis=-1, keepdims=True)
    inverse = lax.rsqrt(jnp.mean(centered * centered, axis=-1, keepdims=True) + epsilon)
    return (centered * inverse, inverse)


def layer_back(normed, inverse, grad_normed):
    mean_grad = jnp.mean(grad_normed, axis=-1, keepdims=True)
    mean_prod = jnp.mean(grad_normed * normed, axis=-1, keepdims=True)
    return inverse * (grad_normed - mean_grad - normed * mean_prod)


def gelu_pair(hidden):
    root = (2.0 / 3.141592653589793) ** 0.5
    square = hidden * hidden
    curve = jnp.tanh(root * (hidden + 0.044715 * square * hidden))
    cdf = 0.5 * (1.0 + curve)
    slope = cdf + 0.5 * hidden * (1.0 - curve * curve) * root * (1.0 + 3 * 0.044715 * square)
    return (hidden * cdf, slope)


def matmul(left, right):
    return jnp.dot(left, right, preferred_element_type=F32)


def matmul_nt(left, right):
    return lax.dot_general(left, right, (((1,), (1,)), ((), ())), preferred_element_type=F32)


def matmul_tn(left, right):
    return lax.dot_general(left, right, (((0,), (0,)), ((), ())), preferred_element_type=F32)


def flip(index, mask):
    return index + mask - 2 * mask * ((index // mask) % 2)


def loop(count, body):
    def step(i, carry):
        body(i)
        return carry

    lax.fori_loop(0, count, step, 0)


def remote(src, dst, send, recv, **device):
    return pltpu.make_async_remote_copy(
        src_ref=src, dst_ref=dst, send_sem=send, recv_sem=recv,
        device_id=device, device_id_type=MESH,
    )


def meet(n, c, me, row):
    barrier = pltpu.get_barrier_semaphore()

    def greet_fsdp(k):
        pl.semaphore_signal(
            barrier, inc=1, device_id={"fsdp": (me + 1 + k) % n}, device_id_type=MESH
        )

    def greet_ctx(k):
        pl.semaphore_signal(
            barrier, inc=1, device_id={"ctx": (row + 1 + k) % c}, device_id_type=MESH
        )

    loop(n - 1, greet_fsdp)
    loop(c - 1, greet_ctx)
    pl.semaphore_wait(barrier, n + c - 2)


def gather_kernel(
    n, c,
    qkv, out, fc1, fc2, tok, cond, ada, ada_bias, small,
    qkv_all, out_all, fc1_all, fc2_all, tok_all, cond_out, mod, small_all,
    cond_all, part, mod_all,
    send_w, recv_w, send_t, recv_t, send_c, recv_c, send_m, recv_m, send_s, recv_s,
):
    me, row = lax.axis_index("fsdp"), lax.axis_index("ctx")
    own = (qkv, out, fc1, fc2)
    full = (qkv_all, out_all, fc1_all, fc2_all)
    stages = n.bit_length() - 1
    meet(n, c, me, row)

    def cond_copy(to, sender):
        return remote(
            cond.at[to], cond_all.at[sender], send_c.at[to], recv_c.at[sender], fsdp=to
        )

    def small_copy(to, sender):
        return remote(small, small_all.at[sender], send_s.at[to], recv_s.at[sender], fsdp=to)

    def mod_copy(to, sender):
        return remote(part.at[to], mod_all.at[sender], send_m.at[to], recv_m.at[sender], fsdp=to)

    def tok_copy(to, sender):
        return remote(tok, tok_all.at[sender], send_t.at[to], recv_t.at[sender], ctx=to)

    def weight_copy(w, s, block, mine):
        return remote(
            own[w] if mine else full[w].at[block],
            full[w].at[block],
            send_w.at[w, s, block],
            recv_w.at[w, block],
            fsdp=flip(me, n >> (s + 1)),
        )

    def others(body):
        loop(n - 1, lambda k: body((me + 1 + k) % n))

    def siblings(body):
        loop(c - 1, lambda k: body((row + 1 + k) % c))

    others(lambda to: cond_copy(to, me).start())
    for w in range(4):
        for s in range(stages):
            weight_copy(w, s, me, True).start()
    others(lambda to: small_copy(to, me).start())
    siblings(lambda to: tok_copy(to, row).start())
    for w in range(4):
        full[w][me] = own[w][...]
    tok_all[row] = tok[...]
    small_all[me] = small[...]
    cond_all[me] = cond[me]
    others(lambda peer: cond_copy(peer, peer).wait_recv())
    lane = lax.broadcasted_iota(jnp.int32, cond_all.shape[1:], 1)
    columns = jnp.zeros(cond_all.shape[1:], F32)
    for i in range(n):
        columns = jnp.where(lane == i, cond_all[i], columns)
    cond_out[...] = columns
    partial_mod = matmul_tn(columns.astype(BF16), ada[...])
    for i in range(n):
        part[i] = partial_mod[i : i + 1, :] + ada_bias[...]
    others(lambda to: mod_copy(to, me).start())
    mod_all[me] = part[me]

    for s in range(stages):
        mask = n >> (s + 1)
        origin = flip(me, mask) % (2 * mask)

        def arrived(t, s=s, mask=mask, origin=origin):
            block = origin + t * (2 * mask)
            for w in range(4):
                weight_copy(w, s, block, False).wait_recv()
                for later in range(s + 1, stages):
                    weight_copy(w, later, block, False).start()

        loop(1 << s, arrived)

    others(lambda peer: mod_copy(peer, peer).wait_recv())
    total = mod_all[0]
    for i in range(1, n):
        total = total + mod_all[i]
    mod[...] = total
    others(lambda peer: small_copy(peer, peer).wait_recv())
    siblings(lambda peer: tok_copy(peer, peer).wait_recv())
    for s in range(stages):
        mask = n >> (s + 1)

        def left(t, s=s, mask=mask):
            block = me % (2 * mask) + t * (2 * mask)
            for w in range(4):
                weight_copy(w, s, block, False).wait_send()

        loop(1 << s, left)
    others(lambda to: cond_copy(to, me).wait_send())
    others(lambda to: small_copy(to, me).wait_send())
    others(lambda to: mod_copy(to, me).wait_send())
    siblings(lambda to: tok_copy(to, row).wait_send())


def vmem(count):
    return [pl.BlockSpec(memory_space=pltpu.VMEM)] * count


def gather(n, c, qkv, out, fc1, fc2, tok, cond, ada, ada_bias, small):
    stages = n.bit_length() - 1
    shape = jax.ShapeDtypeStruct
    dma = pltpu.SemaphoreType.DMA
    return pl.pallas_call(
        partial(gather_kernel, n, c),
        out_shape=[shape((n, *w.shape), BF16) for w in (qkv, out, fc1, fc2)]
        + [
            shape((c, *tok.shape), BF16),
            shape(cond.shape[1:], F32),
            shape(ada_bias.shape, F32),
            shape((n, *small.shape), F32),
        ],
        in_specs=vmem(9),
        out_specs=vmem(8),
        scratch_shapes=[
            pltpu.VMEM(cond.shape, F32),
            pltpu.VMEM((n, *ada_bias.shape), F32),
            pltpu.VMEM((n, *ada_bias.shape), F32),
            dma((4, stages, n)), dma((4, n)),
            dma((c,)), dma((c,)), dma((n,)), dma((n,)), dma((n,)), dma((n,)), dma((n,)), dma((n,)),
        ],
        compiler_params=pltpu.CompilerParams(collective_id=0, has_side_effects=True),
        name="gather",
    )(qkv, out, fc1, fc2, tok, cond, ada, ada_bias, small)


def reduce_kernel(
    n, c,
    qkv, out, fc1, fc2, line, ada, columns, tok, mod, after, hid_own, hid_sent,
    qkv_sum, out_sum, fc1_sum, fc2_sum, grad_input, grad_ada, total_line, back_all,
    *scratch,
):
    stages = n.bit_length() - 1
    me, row = lax.axis_index("fsdp"), lax.axis_index("ctx")
    given = (qkv, out, fc1, fc2)
    sums = (qkv_sum, out_sum, fc1_sum, fc2_sum)
    arrays = len(given)
    incoming = [scratch[w * stages : (w + 1) * stages] for w in range(arrays)]
    scratch = scratch[arrays * stages :]
    kept = [scratch[w * stages : (w + 1) * stages] for w in range(arrays)]
    scratch = scratch[arrays * stages :]
    shares, scratch = scratch[:arrays], scratch[arrays:]
    (gm, gm_ctx, gm_mine, gm_all, back, hid, send_r, recv_r, send_x, recv_x, send_g, recv_g,
     send_f, recv_f, send_b, recv_b, send_h, recv_h) = scratch
    width = tok.shape[1]
    meet(n, c, me, row)

    def others(body):
        loop(n - 1, lambda k: body((me + 1 + k) % n))

    def siblings(body):
        loop(c - 1, lambda k: body((row + 1 + k) % c))

    def ctx_gm(to, sender):
        return remote(gm, gm_ctx.at[sender], send_g.at[to], recv_g.at[sender], ctx=to)

    def fsdp_gm(to, sender):
        return remote(gm_mine, gm_all.at[sender], send_f.at[to], recv_f.at[sender], fsdp=to)

    def back_copy(to, sender):
        return remote(back.at[to], back_all.at[sender], send_b.at[to], recv_b.at[sender], fsdp=to)

    def share_copy(w, to, sender):
        return remote(
            shares[w].at[row], shares[w].at[sender], send_x.at[w, to], recv_x.at[w, sender], ctx=to
        )

    def bit(s):
        return (me // (1 << s)) % 2

    def source(w, s):
        return given[w] if s == 0 else kept[w][s - 1]

    def halve(w, s, j):
        return remote(
            source(w, s).at[2 * j + 1 - bit(s)],
            incoming[w][s].at[j],
            send_r.at[w, s, j],
            recv_r.at[w, s, j],
            fsdp=flip(me, 1 << s),
        )

    def hid_copy(k):
        return remote(
            hid_sent.at[k], hid.at[k], send_h.at[k], recv_h.at[k], ctx=(row + 1 + k) % c
        )

    for k in range(c - 1):
        hid_copy(k).start()

    def send_all(s, base, step, count):
        def body(t):
            for w in range(arrays):
                halve(w, s, base + step * t).start()

        loop(count, body)

    send_all(0, 1 - bit(1), 2, n // 4)
    send_all(0, bit(1), 2, n // 4)

    normed, inverse = layer_stats(tok[...].astype(F32))
    grad_hidden = hid_own[...]
    for k in range(c - 1):
        hid_copy(k).wait_recv()
        grad_hidden = grad_hidden + hid[k].astype(F32)
    grad_input[...] = (
        after[...]
        + layer_back(normed, inverse, grad_hidden * (1.0 + mod[:, width : 2 * width]))
    ).astype(BF16)
    gm[:, :width] = jnp.sum(grad_hidden, axis=0, keepdims=True)
    gm[:, width : 2 * width] = jnp.sum(grad_hidden * normed, axis=0, keepdims=True)
    gm[:, 2 * width :] = line[:, 2 * width :]
    siblings(lambda to: ctx_gm(to, row).start())
    gm_ctx[row] = gm[...]
    siblings(lambda peer: ctx_gm(peer, peer).wait_recv())
    total = gm_ctx[0]
    for i in range(1, c):
        total = total + gm_ctx[i]
    gm_mine[...] = total
    gm_all[me] = total
    others(lambda to: fsdp_gm(to, me).start())

    def backward():
        others(lambda peer: fsdp_gm(peer, peer).wait_recv())
        rows = lax.broadcasted_iota(jnp.int32, (n, gm.shape[1]), 0)
        stacked = jnp.zeros((n, gm.shape[1]), F32)
        for i in range(n):
            stacked = jnp.where(rows == i, jnp.broadcast_to(gm_all[i], stacked.shape), stacked)
        wide = 6 * width
        total_line[...] = jnp.sum(stacked, axis=0, keepdims=True)
        grad_ada[...] = lax.dot_general(
            columns[...][:, :n], stacked[:, :wide], (((1,), (0,)), ((), ())),
            preferred_element_type=F32, precision=lax.Precision.HIGHEST,
        )
        product = lax.dot_general(
            stacked[:, :wide], ada[...], (((1,), (1,)), ((), ())),
            preferred_element_type=F32, precision=lax.Precision.HIGHEST,
        )
        for i in range(n):
            back[i] = product[i : i + 1, :]
        others(lambda to: back_copy(to, me).start())
        back_all[me] = back[me]

    def add(w, s, j):
        halve(w, s, j).wait_recv()
        value = source(w, s)[2 * j + bit(s)].astype(F32) + incoming[w][s][j].astype(F32)
        if s == stages - 1:
            shares[w][row] = value.astype(given[w].dtype)
        else:
            kept[w][s][j] = value.astype(given[w].dtype)

    for s in range(stages):
        if s == stages - 1:
            for w in range(arrays):
                add(w, s, 0)
                siblings(lambda to, w=w: share_copy(w, to, row).start())
            continue

        def first(t, s=s):
            j = 2 * t + 1 - bit(s + 1)
            for w in range(arrays):
                add(w, s, j)
                halve(w, s + 1, t).start()

        def second(t, s=s):
            for w in range(arrays):
                add(w, s, 2 * t + bit(s + 1))

        loop(n >> (s + 2), first)
        loop(n >> (s + 2), second)
        if s == 0:
            backward()

    for w in range(arrays):
        siblings(lambda peer, w=w: share_copy(w, peer, peer).wait_recv())
        value = shares[w][0].astype(F32)
        for i in range(1, c):
            value = value + shares[w][i].astype(F32)
        sums[w][...] = value
    others(lambda peer: back_copy(peer, peer).wait_recv())

    for k in range(c - 1):
        hid_copy(k).wait_send()
    siblings(lambda to: ctx_gm(to, row).wait_send())
    others(lambda to: fsdp_gm(to, me).wait_send())
    others(lambda to: back_copy(to, me).wait_send())
    for s in range(stages):

        def sent(j, s=s):
            for w in range(arrays):
                halve(w, s, j).wait_send()

        loop(n >> (s + 1), sent)
    for w in range(arrays):
        siblings(lambda to, w=w: share_copy(w, to, row).wait_send())


def reduce(n, c, qkv, out, fc1, fc2, line, ada, columns, tok, mod, after, hid_own, hid_sent):
    stages = n.bit_length() - 1
    shape = jax.ShapeDtypeStruct
    dma = pltpu.SemaphoreType.DMA
    given = (qkv, out, fc1, fc2)
    halves = [
        pltpu.VMEM((n >> (s + 1), *w.shape[1:]), w.dtype) for w in given for s in range(stages)
    ]
    back = (n, 1, ada.shape[0])
    return pl.pallas_call(
        partial(reduce_kernel, n, c),
        out_shape=[shape(w.shape[1:], F32) for w in given]
        + [
            shape(tok.shape, BF16),
            shape((columns.shape[0], mod.shape[1]), F32),
            shape(line.shape, F32),
            shape(back, F32),
        ],
        in_specs=vmem(12),
        out_specs=vmem(8),
        scratch_shapes=halves
        + halves
        + [pltpu.VMEM((c, *w.shape[1:]), w.dtype) for w in given]
        + [
            pltpu.VMEM(line.shape, F32),
            pltpu.VMEM((c, *line.shape), F32),
            pltpu.VMEM(line.shape, F32),
            pltpu.VMEM((n, *line.shape), F32),
            pltpu.VMEM(back, F32),
            pltpu.VMEM(hid_sent.shape, BF16),
            dma((4, stages, n // 2)), dma((4, stages, n // 2)),
            dma((4, c)), dma((4, c)), dma((c,)), dma((c,)),
            dma((n,)), dma((n,)), dma((n,)), dma((n,)), dma((c,)), dma((c,)),
        ],
        compiler_params=pltpu.CompilerParams(collective_id=1, has_side_effects=True),
        name="reduce",
    )(qkv, out, fc1, fc2, line, ada, columns, tok, mod, after, hid_own, hid_sent)


def head(array, h):
    return array[:, h * HEAD : (h + 1) * HEAD]


def block_kernel(
    c,
    qkv_ref, out_ref, fc1_ref, fc2_ref, tok_ref, mod_ref, bias_ref, cot_ref,
    result_ref, after_ref, hid_own_ref, hid_sent_ref, qkv_grad, out_grad, fc1_grad, fc2_grad,
    line_ref,
):
    width = cot_ref.shape[1]
    rows = cot_ref.shape[0]
    hidden_width = fc1_ref.shape[1]
    scale_factor = HEAD ** (-0.5)
    shift_one, scale_one, gate_one, shift_two, scale_two, gate_two = (
        mod_ref[:, k * width : (k + 1) * width] for k in range(6)
    )
    starts = (0, width, 2 * width, 3 * width, 3 * width + hidden_width, 4 * width + hidden_width)
    query_bias, value_bias, out_bias, fc1_bias, fc2_bias = (
        bias_ref[:, a:b] for a, b in zip(starts, starts[1:])
    )
    residual_all = tok_ref[...].astype(F32)
    normed_all, _ = layer_stats(residual_all)
    hidden_all = (normed_all * (1.0 + scale_one) + shift_one).astype(BF16)
    residual, hidden_one = residual_all[:rows], hidden_all[:rows]
    queries = (matmul(hidden_one, qkv_ref[:, :width]) + query_bias).astype(BF16)
    keys = matmul(hidden_all, qkv_ref[:, width : 2 * width]).astype(BF16)
    values = (matmul(hidden_all, qkv_ref[:, 2 * width :]) + value_bias).astype(BF16)
    probabilities, mixed_heads = [], []
    for h in range(HEADS):
        scores = matmul_nt(head(queries, h), head(keys, h)) * scale_factor
        raised = jnp.exp(scores - jnp.max(scores, axis=1, keepdims=True))
        probability = raised * (1.0 / jnp.sum(raised, axis=1, keepdims=True))
        probabilities.append(probability)
        mixed_heads.append(matmul(probability.astype(BF16), head(values, h)))
    mixed = jnp.concatenate(mixed_heads, axis=1).astype(BF16)
    attn_out = matmul(mixed, out_ref[...]) + out_bias
    after_attn = residual + gate_one * attn_out
    normed_two, inverse_two = layer_stats(after_attn)
    hidden_two = (normed_two * (1.0 + scale_two) + shift_two).astype(BF16)
    pre_act = matmul(hidden_two, fc1_ref[...]) + fc1_bias
    activated, slope = gelu_pair(pre_act)
    activated = activated.astype(BF16)
    mlp_out = matmul(activated, fc2_ref[...]) + fc2_bias
    result_ref[...] = (after_attn + gate_two * mlp_out).astype(BF16)

    def total(array):
        return jnp.sum(array, axis=0, keepdims=True)

    grad_result = cot_ref[...].astype(F32)
    grad_mlp_float = grad_result * gate_two
    grad_mlp = grad_mlp_float.astype(BF16)
    fc2_grad[...] = matmul_tn(activated, grad_mlp).astype(BF16)
    grad_pre = slope * matmul_nt(grad_mlp, fc2_ref[...])
    grad_pre_half = grad_pre.astype(BF16)
    fc1_grad[...] = matmul_tn(hidden_two, grad_pre_half).astype(BF16)
    grad_hidden_two = matmul_nt(grad_pre_half, fc1_ref[...])
    grad_after = grad_result + layer_back(
        normed_two, inverse_two, grad_hidden_two * (1.0 + scale_two)
    )
    after_ref[...] = grad_after
    grad_attn_float = grad_after * gate_one
    grad_attn = grad_attn_float.astype(BF16)
    out_grad[...] = matmul_tn(mixed, grad_attn).astype(BF16)
    grad_mixed = matmul_nt(grad_attn, out_ref[...]).astype(BF16)
    grad_q, grad_k, grad_v = [], [], []
    for h in range(HEADS):
        grad_head = head(grad_mixed, h)
        inner = jnp.sum(
            grad_head.astype(F32) * head(mixed, h).astype(F32), axis=1, keepdims=True
        )
        grad_prob = matmul_nt(grad_head, head(values, h))
        grad_scores = (probabilities[h] * (grad_prob - inner) * scale_factor).astype(BF16)
        grad_q.append(matmul(grad_scores, head(keys, h)))
        grad_k.append(matmul_tn(grad_scores, head(queries, h)))
        grad_v.append(matmul_tn(probabilities[h].astype(BF16), grad_head))
    grad_query = jnp.concatenate(grad_q, axis=1)
    grad_value = jnp.concatenate(grad_v, axis=1)
    grad_kv = jnp.concatenate(grad_k + grad_v, axis=1).astype(BF16)
    query_half = grad_query.astype(BF16)
    hid_kv = matmul_nt(grad_kv, qkv_ref[:, width:])
    hid_own_ref[...] = hid_kv[:rows] + matmul_nt(query_half, qkv_ref[:, :width])
    for k in range(1, c):
        hid_sent_ref[k - 1] = hid_kv[k * rows : (k + 1) * rows].astype(BF16)
    qkv_grad[:, :width] = matmul_tn(hidden_one, query_half).astype(BF16)
    qkv_grad[:, width:] = matmul_tn(hidden_all, grad_kv).astype(BF16)
    line = (
        jnp.zeros((1, 2 * width), F32),
        total(grad_after * attn_out),
        total(grad_hidden_two),
        total(grad_hidden_two * normed_two),
        total(grad_result * mlp_out),
        total(grad_query),
        total(grad_value),
        total(grad_attn_float),
        total(grad_pre),
        total(grad_mlp_float),
    )
    start = 0
    for piece in line:
        line_ref[:, start : start + piece.shape[1]] = piece
        start += piece.shape[1]


def block(c, qkv, out, fc1, fc2, tok, mod, bias, cot):
    shape = jax.ShapeDtypeStruct
    return pl.pallas_call(
        partial(block_kernel, c),
        out_shape=[
            shape(cot.shape, BF16),
            shape(cot.shape, F32),
            shape(cot.shape, F32),
            shape((c - 1, *cot.shape), BF16),
            shape(qkv.shape, BF16),
            shape(out.shape, BF16),
            shape(fc1.shape, BF16),
            shape(fc2.shape, BF16),
            shape((1, mod.shape[1] + bias.shape[1]), F32),
        ],
        in_specs=vmem(8),
        out_specs=vmem(9),
        name="block",
    )(qkv, out, fc1, fc2, tok, mod, bias, cot)


def per_device(
    n, c,
    tokens, condition,
    ada_weight, ada_bias, qkv_weight, qv_bias, out_weight, out_bias,
    fc1_weight, fc1_bias, fc2_weight, fc2_bias,
    cotangent,
):
    latents, local_rows, width = tokens.shape
    me, row = lax.axis_index("fsdp"), lax.axis_index("ctx")
    scale_factor = HEAD ** (-0.5)
    tok = tokens[0]
    slice_rows = ada_weight.shape[0]
    cond_float = condition.astype(F32)
    cond_silu = jax.nn.silu(cond_float).astype(BF16)
    cond_columns = jnp.broadcast_to(
        cond_silu.astype(F32).reshape(n, slice_rows, 1), (n, slice_rows, 128)
    )
    bias_row = lax.dynamic_update_slice(
        jnp.zeros((1, ada_bias.shape[0] * n), F32),
        ada_bias.astype(F32)[None, :],
        (0, me * ada_bias.shape[0]),
    )
    biases = jnp.concatenate([qv_bias, out_bias, fc1_bias, fc2_bias]).astype(F32)
    small = jnp.pad(biases, (0, 256 - biases.shape[0]))[None, :]
    qkv_all, out_all, fc1_all, fc2_all, tok_all, columns, modulation, small_all = gather(
        n, c, qkv_weight, out_weight, fc1_weight, fc2_weight, tok, cond_columns,
        ada_weight, bias_row, small,
    )
    pieces, start = [], 0
    for piece in (qv_bias, out_bias, fc1_bias, fc2_bias):
        pieces.append(small_all[:, 0, start : start + piece.shape[0]].reshape(1, -1))
        start += piece.shape[0]
    order = [lax.rem(row + k, c) for k in range(c)]
    rotated = jnp.concatenate([tok] + [tok_all[i] for i in order[1:]], axis=0)
    result, after, hid_own, hid_sent, grad_qkv, grad_out, grad_fc1, grad_fc2, line = block(
        c,
        qkv_all.reshape(-1, qkv_weight.shape[1]),
        out_all.reshape(-1, width),
        fc1_all.reshape(-1, fc1_weight.shape[1]),
        fc2_all.reshape(-1, width),
        rotated, modulation, jnp.concatenate(pieces, axis=1), cotangent[0],
    )
    ada_rows = jnp.pad(ada_weight.astype(F32), ((0, 128 - slice_rows), (0, 0)))
    qkv_sum, out_sum, fc1_sum, fc2_sum, grad_input, grad_ada_w, total_line, back_all = reduce(
        n, c,
        grad_qkv.reshape(qkv_all.shape),
        grad_out.reshape(out_all.shape),
        grad_fc1.reshape(fc1_all.shape),
        grad_fc2.reshape(fc2_all.shape),
        line, ada_rows, columns, tok, modulation, after, hid_own, hid_sent,
    )
    ada_back_term = back_all[:, 0, :slice_rows].reshape(1, -1)
    grad_cond = jax.vjp(jax.nn.silu, cond_float)[1](ada_back_term)[0]
    parts, start = [], 0
    for piece in (ada_bias, qv_bias, out_bias, fc1_bias, fc2_bias):
        size = piece.shape[0]
        parts.append(lax.dynamic_slice(total_line, (0, start + me * size), (1, size))[0])
        start += n * size
    return (
        result[None], grad_input[None], grad_cond,
        grad_ada_w, parts[0],
        qkv_sum, parts[1], out_sum, parts[2], fc1_sum, parts[3], fc2_sum, parts[4],
    )


def solution(mesh):
    n, c = mesh.shape["fsdp"], mesh.shape["ctx"]
    return jax.shard_map(
        partial(per_device, n, c),
        mesh=mesh,
        in_specs=(
            P("fsdp", "ctx", None),
            P("fsdp", None),
            P("fsdp", None),
            P("fsdp"),
            P("fsdp", None),
            P("fsdp"),
            P("fsdp", None),
            P("fsdp"),
            P("fsdp", None),
            P("fsdp"),
            P("fsdp", None),
            P("fsdp"),
            P("fsdp", "ctx", None),
        ),
        out_specs=(
            P("fsdp", "ctx", None),
            P("fsdp", "ctx", None),
            P("fsdp", None),
            P("fsdp", None),
            P("fsdp"),
            P("fsdp", None),
            P("fsdp"),
            P("fsdp", None),
            P("fsdp"),
            P("fsdp", None),
            P("fsdp"),
            P("fsdp", None),
            P("fsdp"),
        ),
        check_vma=False,
    )
```
